32 devices in a mesh: grp: 2 (over core), tile: 16 (over z, y, x).
Axes of the slice: x: 2, y: 2, z: 4, core: 2. Of those that a mesh axis runs over, the one named last changes fastest.
Arguments:
- source_points: float32 [2, 3, 524288], P('grp', None, 'tile'), may hold values from -6 to 6
- intersection: int32 [2, 2048, 1], P('grp', 'tile'), may hold values from 0 to 15; in each aligned block of 128 rows (0 to 127, 128 to 255, ..., all dimensions but the last counted through in order) at most 16 rows name the same one
- target_scan: int32 [2, 2048], P('grp', 'tile'), may hold values from 0 to 63
- matches: int32 [2, 524288], P('grp', 'tile'), may hold values from 0 to 511
- target_points: float32 [3, 524288], P(None, 'tile'), may hold values from -6 to 6
- target_normals: float32 [3, 524288], P(None, 'tile'), may hold values from -4 to 4
Outputs:
- pose_step: float32 [6, 1024], P(None, 'tile')
The draws below stay inside these ranges and needn't reach their ends.
Inputs may be any that keep to these rules, and one draw needn't show every extreme that they name: `intersection`: within the blocks of one device (each aligned run of 128 rows), no index is named more than 16 times, a bound that some block reaches.
All inputs are finite; a program needn't handle non-finite values.
Results may differ from the reference program's by a relative error of at most 0.0003.
Values sent between devices are 32-bit elements; how exact they have to be, the bound alone decides.
No kernel may reach another device: no remote copies, remote signals or barrier semaphores. Data moves between devices by JAX's collectives and lax.ppermute only.
A program may use at most 64 MiB of HBM per device.

```python
import math
import jax
import jax.numpy as jnp
import numpy as np
from jax import lax

BLOCK_PTS = 256
BLOCKS_DEV = 128
SCANS_DEV = 64
TARGET_PTS = 512
CAP = 16
GRPS = 2
BLOCKS = 2048
SCANS = 1024
TILE_PTS = 524288
N_TILE = 16


def set_ends(array, stream_key, least, top_value):
    longest = array.shape.index(max(array.shape))
    spots = []
    for shift in (0, 1):
        where = [jax.random.randint(jax.random.fold_in(stream_key, axis), (), 0, length) for axis, length in enumerate(array.shape)]
        where[longest] = (where[longest] + shift) % array.shape[longest]
        spots.append(tuple(where))
    return array.at[spots[0]].set(least).at[spots[1]].set(top_value)


def shard_levels(stream_key, shape, shards, smallest, high):
    def one(axis_at, parts):
        steps = jax.random.uniform(jax.random.fold_in(jax.random.fold_in(stream_key, 6), axis_at), (parts,), jnp.float32, smallest / len(shards), high / len(shards))
        return jnp.repeat(jnp.exp(steps), shape[axis_at] // parts).reshape((-1,) + (1,) * (len(shape) - axis_at - 1))

    level = one(*shards[0])
    for cut in shards[1:]:
        level = level * one(*cut)
    return level


def routed_block(own_key, own, number, rows, amount, top, limit, skew):
    order = jax.random.permutation(own_key, amount)
    crowded, usual = shares(amount, rows * top, limit, skew, True), shares(amount, rows * top, limit, skew, False)
    places = jnp.arange(amount)

    def named(tallies, rotation):
        used = int((tallies > 0).sum())
        fixed = max(1, used // 4)
        passed = fixed + (places - fixed + rotation * (used - fixed)) % max(1, amount - fixed)
        return jnp.zeros((amount,), jnp.int32).at[order[jnp.where(places < fixed, places, passed)]].set(jnp.asarray(tallies, jnp.int32))

    tallies = jnp.where(number % 4 == 0, named(crowded, number // 4), named(usual, number - number // 4 - 1))
    mixed = jax.random.permutation(jax.random.fold_in(own, 3), amount)
    source_of, sink = mixed[0:amount // 2 * 2:2], mixed[1:amount // 2 * 2:2]
    slack = jnp.minimum(tallies[source_of] - 1, limit - tallies[sink]) // 2
    slack = jnp.where((source_of == order[0]) | (sink == order[0]) | (tallies[sink] == 0), 0, jnp.maximum(slack, 0))
    passed = jax.random.randint(jax.random.fold_in(own, 4), (amount // 2,), 0, 1 << 20) % (slack + 1)
    tallies = tallies.at[source_of].add(-passed).at[sink].add(passed)
    members = jnp.searchsorted(jnp.cumsum(tallies), jnp.arange(rows * top), side="right").astype(jnp.int32)
    grid = members.reshape(top, rows).T
    grid = grid[jax.random.permutation(jax.random.fold_in(own, 1), rows)]
    rotation = jax.random.randint(jax.random.fold_in(own, 2), (rows, 1), 0, top)
    return jnp.take_along_axis(grid, (jnp.arange(top)[None, :] + rotation) % top, axis=1)


def shares(amount, total, most, lean, full):
    loads = [(1 << 20) // math.isqrt(grade ** lean) + 1 for grade in range(1, amount + 1)]
    largest = most if full else min(most, max(-(-total // amount), total * loads[0] // sum(loads)))
    least = 1 if total - largest >= amount - 1 else 0
    given, spare = [largest] + [least] * (amount - 1), total - largest - least * (amount - 1)
    while spare > 0:
        movable = [i for i in range(1, amount) if given[i] < largest] or [i for i in range(1, amount) if given[i] < most]
        pool, left = sum([loads[i] for i in movable]), spare
        for i in movable:
            more = min(most - given[i], max(1, left * loads[i] // pool), spare)
            given[i] = given[i] + more
            spare = spare - more
    return np.array(given)


def gaussian(key, extent, width, reach, pieces=(), kind=jnp.bfloat16):
    drawn = jax.random.normal(key, extent, jnp.float32) * width
    if len(pieces) > 0:
        drawn = shard_levels(key, extent, pieces, -0.22, 0.18) * drawn
    return jnp.clip(drawn, min=-reach, max=reach).astype(kind)


def setup_inputs(seed: int = 0) -> dict:
    keys = jax.random.split(jax.random.key(seed), 7)
    source_points = gaussian(keys[0], (GRPS, 3, BLOCKS * BLOCK_PTS), 1.0, 6.0, ((0, 2), (2, 16)), jnp.float32)
    intersection_keys = jax.random.split(jax.random.fold_in(keys[1], 1), GRPS * BLOCKS // BLOCKS_DEV)
    intersection_turns = jax.random.permutation(jax.random.fold_in(keys[1], 3), GRPS * BLOCKS // BLOCKS_DEV)
    intersection = jax.vmap(lambda own, number: routed_block(jax.random.fold_in(keys[1], 2), own, number, BLOCKS_DEV, N_TILE, 1, CAP, 2))(intersection_keys, intersection_turns).reshape((GRPS, BLOCKS, 1))
    target_scan = set_ends(jax.random.randint(keys[2], (GRPS, BLOCKS), 0, SCANS_DEV), jax.random.fold_in(keys[2], 1), 0, SCANS_DEV - 1).astype(jnp.int32)
    matches = set_ends(jax.random.randint(keys[3], (GRPS, BLOCKS * BLOCK_PTS), 0, TARGET_PTS), jax.random.fold_in(keys[3], 1), 0, TARGET_PTS - 1).astype(jnp.int32)
    target_points = gaussian(keys[4], (3, TILE_PTS), 1.0, 6.0, ((1, 16),), jnp.float32)
    target_normals = gaussian(keys[5], (3, TILE_PTS), 0.6, 4.0, ((1, 16),), jnp.float32)
    return {"source_points": source_points, "intersection": intersection, "target_scan": target_scan, "matches": matches, "target_points": target_points, "target_normals": target_normals}


DAMPING = 0.1
PRECISE = lax.Precision.HIGHEST


def cross_rows(first_vec, second_vec):
    return jnp.stack([first_vec[1] * second_vec[2] - first_vec[2] * second_vec[1],
                      first_vec[2] * second_vec[0] - first_vec[0] * second_vec[2],
                      first_vec[0] * second_vec[1] - first_vec[1] * second_vec[0]])


def pair_terms(source, target, normal, usable):
    jacobian = jnp.concatenate([cross_rows(source, normal), normal, -cross_rows(target, normal), -normal], axis=0) * usable[None]
    misfit = jnp.sum(normal * (source - target), axis=0) * usable
    normal_blocks = jnp.einsum("anks,bnks->abnk", jacobian, jacobian, precision=PRECISE)
    gradient = jnp.einsum("anks,nks->ank", jacobian, misfit, precision=PRECISE)
    layout = jacobian.shape[1:3]
    own_terms = jnp.concatenate([normal_blocks[:6, :6].reshape((36,) + layout), gradient[:6]], axis=0)
    theirs = jnp.concatenate([normal_blocks[6:, 6:].reshape((36,) + layout), gradient[6:]], axis=0)
    return own_terms, theirs


def solve_poses(scan_totals):
    entries = [[scan_totals[6 * row_at + col_at] for col_at in range(6)] for row_at in range(6)]
    traced = entries[0][0]
    for step_at in range(1, 6):
        traced = traced + entries[step_at][step_at]
    shift_by = DAMPING * traced / 6.0
    for step_at in range(6):
        entries[step_at][step_at] = entries[step_at][step_at] + shift_by
    values = [-scan_totals[36 + row_at] for row_at in range(6)]
    for pivot_at in range(6):
        for row_at in range(pivot_at + 1, 6):
            factor = entries[row_at][pivot_at] / entries[pivot_at][pivot_at]
            for col_at in range(pivot_at, 6):
                entries[row_at][col_at] = entries[row_at][col_at] - factor * entries[pivot_at][col_at]
            values[row_at] = values[row_at] - factor * values[pivot_at]
    result = [None] * 6
    for row_at in range(5, -1, -1):
        running = values[row_at]
        for col_at in range(row_at + 1, 6):
            running = running - entries[row_at][col_at] * result[col_at]
        result[row_at] = running / entries[row_at][row_at]
    return jnp.stack(result)


def reference(source_points, intersection, target_scan, matches, target_points, target_normals):
    per_scan = BLOCKS_DEV // SCANS_DEV
    block_span = BLOCKS_DEV * BLOCK_PTS
    tile_span = SCANS_DEV * TARGET_PTS
    anchor = jnp.int32(0)

    def accumulate(totals, stretch_at):
        grp_at = (stretch_at // N_TILE).astype(jnp.int32)
        tile_at = (stretch_at % N_TILE).astype(jnp.int32)
        coords = lax.dynamic_slice(source_points, (grp_at, anchor, tile_at * block_span), (1, 3, block_span))[0]
        coords = coords.reshape(3, 1, BLOCKS_DEV, BLOCK_PTS)
        destin = lax.dynamic_slice(intersection, (grp_at, tile_at * BLOCKS_DEV, anchor), (1, BLOCKS_DEV, 1))[0, :, 0]
        chosen = lax.dynamic_slice(target_scan, (grp_at, tile_at * BLOCKS_DEV), (1, BLOCKS_DEV))[0]
        picked = lax.dynamic_slice(matches, (grp_at, tile_at * block_span), (1, block_span))[0].reshape(BLOCKS_DEV, BLOCK_PTS)
        target_index = (destin[:, None] * tile_span + chosen[:, None] * TARGET_PTS + picked).astype(jnp.int32)
        nearest = jnp.take(target_points, target_index, axis=1)[:, None]
        facing = jnp.take(target_normals, target_index, axis=1)[:, None]
        usable = jnp.ones((1, BLOCKS_DEV, BLOCK_PTS), jnp.float32)
        own_terms, theirs = pair_terms(coords, nearest, facing, usable)
        source_ids = (tile_at * SCANS_DEV + jnp.arange(BLOCKS_DEV, dtype=jnp.int32) // per_scan).astype(jnp.int32)
        target_ids = (destin * SCANS_DEV + chosen).astype(jnp.int32)
        totals = totals + jax.ops.segment_sum(own_terms[:, 0].T, source_ids, num_segments=SCANS).T
        totals = totals + jax.ops.segment_sum(theirs[:, 0].T, target_ids, num_segments=SCANS).T
        return totals, None

    totals, unused = lax.scan(accumulate, jnp.zeros((42, SCANS), jnp.float32), jnp.arange(GRPS * N_TILE, dtype=jnp.int32))
    return solve_poses(totals)
```

```python
import functools

import jax
import jax.numpy as jnp
from jax import lax
from jax.experimental import pallas as pl
from jax.experimental.pallas import tpu as pltpu
from jax.sharding import PartitionSpec as P

SCANS_DEV = 64
TARGET_PTS = 512
LANES = 128
GROUP = 8
HALF = 32

DAMPING = 0.1
PRECISE = lax.Precision.HIGHEST
PAIRS = [(r, c) for r in range(6) for c in range(r, 6)]
PAIR_AT = {pair: at for at, pair in enumerate(PAIRS)}


def pack_kernel(
    dest_ref, scan_ref, points_ref, matches_ref, out_ref, slot_scan_ref, count_ref, *, capacity, blocks, points
):
    tiles = count_ref.shape[0]
    halves = points // LANES
    slots = tiles * capacity
    per_scan = blocks // SCANS_DEV
    out_ref[...] = jnp.full(out_ref.shape, -1.0, jnp.float32)

    def clear_count(at, carry):
        count_ref[at] = 0
        return carry

    def clear_slot(at, carry):
        slot_scan_ref[at] = -1
        return carry

    lax.fori_loop(0, tiles, clear_count, 0, unroll=8)
    lax.fori_loop(0, slots, clear_slot, 0, unroll=8)

    def place(block, carry):
        dest = dest_ref[block]
        rank = count_ref[dest]
        count_ref[dest] = rank + 1
        slot = dest * capacity + rank
        slot_scan_ref[slot] = block // per_scan
        base = pl.multiple_of(slot * (4 * halves), 8)
        for half in range(halves):
            start = pl.multiple_of(block * points + half * LANES, LANES)
            span = pl.ds(start, LANES)
            out_ref[pl.ds(base + half * 4, 3), :] = points_ref[0, :, span]
            wanted = matches_ref[:, span] + scan_ref[block] * TARGET_PTS
            out_ref[pl.ds(base + half * 4 + 3, 1), :] = wanted.astype(jnp.float32)
        return carry

    lax.fori_loop(0, blocks, place, 0, unroll=4)


def cross(first, second):
    return [
        first[1] * second[2] - first[2] * second[1],
        first[2] * second[0] - first[0] * second[2],
        first[0] * second[1] - first[1] * second[0],
    ]


def pair_kernel(scan_ref, x_ref, table_ref, out_ref, picked_ref, *, points):
    groups = out_ref.shape[0] // GROUP
    halves = points // LANES
    chunks = TARGET_PTS // LANES
    lane = lax.broadcasted_iota(jnp.int32, (GROUP, LANES), 1)

    def one_group(group, carry):
        base = pl.multiple_of(group * (4 * halves * GROUP), 8)

        def field(comp):
            parts = [x_ref[pl.ds(base + 4 * half + comp, GROUP, stride=4 * halves), :] for half in range(halves)]
            return jnp.concatenate(parts, axis=1)

        def chosen(comp):
            parts = [picked_ref[pl.ds(half * 8 * GROUP + comp, GROUP, stride=8), :] for half in range(halves)]
            return jnp.concatenate(parts, axis=1)

        index = field(3).astype(jnp.int32)
        valid = index >= 0
        low = index & (LANES - 1)
        high = (index >> 7) & (chunks - 1)
        for item in range(GROUP):
            scan = jnp.maximum(scan_ref[group * GROUP + item], 0)
            start = pl.multiple_of(scan * TARGET_PTS, TARGET_PTS)
            parts = [
                table_ref[:, pl.ds(pl.multiple_of(start + at * LANES, LANES), LANES)] for at in range(chunks)
            ]
            for half in range(halves):
                span = slice(half * LANES, (half + 1) * LANES)
                low_at = jnp.broadcast_to(low[item : item + 1, span], (8, LANES))
                high_at = jnp.broadcast_to(high[item : item + 1, span], (8, LANES))
                found = jnp.take_along_axis(parts[0], low_at, axis=1, mode="promise_in_bounds")
                for at in range(1, chunks):
                    other = jnp.take_along_axis(parts[at], low_at, axis=1, mode="promise_in_bounds")
                    found = jnp.where(high_at == at, other, found)
                picked_ref[pl.ds((half * GROUP + item) * 8, 8), :] = found
        p = [field(comp) for comp in range(3)]
        q = [chosen(comp) for comp in range(3)]
        n = [jnp.where(valid, chosen(comp), 0.0) for comp in range(3, 6)]
        misfit = n[0] * (p[0] - q[0]) + n[1] * (p[1] - q[1]) + n[2] * (p[2] - q[2])
        own = cross(p, n) + n
        far = cross(q, n) + n

        def total(product):
            folded = product[:, :LANES]
            for half in range(1, halves):
                folded = folded + product[:, half * LANES : (half + 1) * LANES]
            return jnp.sum(folded, axis=1, keepdims=True)

        result = jnp.zeros((GROUP, LANES), jnp.float32)
        for at, (r, c) in enumerate(PAIRS):
            mine = total(own[r] * own[c])
            result = jnp.where(lane == at, mine, result)
            theirs = mine if r >= 3 else total(far[r] * far[c])
            result = jnp.where(lane == HALF + at, theirs, result)
        for at in range(6):
            mine = total(own[at] * misfit)
            result = jnp.where(lane == 21 + at, mine, result)
            theirs = mine if at >= 3 else total(far[at] * misfit)
            result = jnp.where(lane == HALF + 21 + at, -theirs, result)
        out_ref[pl.ds(pl.multiple_of(group * GROUP, GROUP), GROUP), :] = result
        return carry

    lax.fori_loop(0, groups, one_group, 0)


def solve_poses(totals):
    entries = [[totals[PAIR_AT[min(r, c), max(r, c)]] for c in range(6)] for r in range(6)]
    traced = entries[0][0]
    for at in range(1, 6):
        traced = traced + entries[at][at]
    shift_by = DAMPING * traced / 6.0
    for at in range(6):
        entries[at][at] = entries[at][at] + shift_by
    values = [-totals[21 + at] for at in range(6)]
    for pivot in range(6):
        for row in range(pivot + 1, 6):
            factor = entries[row][pivot] / entries[pivot][pivot]
            for col in range(pivot, 6):
                entries[row][col] = entries[row][col] - factor * entries[pivot][col]
            values[row] = values[row] - factor * values[pivot]
    result = [None] * 6
    for row in range(5, -1, -1):
        running = values[row]
        for col in range(row + 1, 6):
            running = running - entries[row][col] * result[col]
        result[row] = running / entries[row][row]
    return jnp.stack(result)


def body(source_points, intersection, target_scan, matches, target_points, target_normals):
    tiles = lax.axis_size("tile")
    blocks = intersection.shape[1]
    capacity = 2 * blocks // tiles
    slots = tiles * capacity
    points = source_points.shape[2] // blocks
    vmem = pl.BlockSpec(memory_space=pltpu.VMEM)
    smem = pl.BlockSpec(memory_space=pltpu.SMEM)
    message, slot_scan = pl.pallas_call(
        functools.partial(pack_kernel, capacity=capacity, blocks=blocks, points=points),
        out_shape=(
            jax.ShapeDtypeStruct((slots * 4 * points // LANES, LANES), jnp.float32),
            jax.ShapeDtypeStruct((slots,), jnp.int32),
        ),
        in_specs=[smem, smem, vmem, vmem],
        out_specs=(vmem, smem),
        scratch_shapes=[pltpu.SMEM((tiles,), jnp.int32)],
        name="pack",
    )(intersection.reshape(blocks), target_scan.reshape(blocks), source_points, matches)
    incoming = lax.all_to_all(message, "tile", split_axis=0, concat_axis=0, tiled=True)
    pad = jnp.zeros((2, target_points.shape[1]), jnp.float32)
    tables = jnp.concatenate([target_points, target_normals, pad], axis=0)
    leading = incoming.reshape(slots, 4 * points // LANES, LANES)[:, 3, 0].astype(jnp.int32)
    owner_scan = leading >> 9
    terms = pl.pallas_call(
        functools.partial(pair_kernel, points=points),
        out_shape=jax.ShapeDtypeStruct((slots, LANES), jnp.float32),
        in_specs=[smem, vmem, vmem],
        out_specs=vmem,
        scratch_shapes=[pltpu.VMEM((GROUP * 8 * points // LANES, LANES), jnp.float32)],
        name="pairs",
    )(owner_scan, incoming, tables)
    returned = lax.all_to_all(terms, "tile", split_axis=0, concat_axis=0, tiled=True)
    scans = jnp.arange(SCANS_DEV, dtype=jnp.int32)
    src_onehot = (slot_scan[:, None] == scans[None, :]).astype(jnp.float32)
    tgt_onehot = (owner_scan[:, None] == scans[None, :]).astype(jnp.float32)
    contract = (((0,), (0,)), ((), ()))
    far_sums = lax.dot_general(terms[:, HALF : 2 * HALF], tgt_onehot, contract, precision=PRECISE)
    sums = lax.dot_general(returned[:, :HALF], src_onehot, contract, precision=PRECISE) + far_sums
    totals = lax.psum(sums, "grp")
    return solve_poses(totals)


def solution(mesh):
    in_specs = (
        P("grp", None, "tile"),
        P("grp", "tile", None),
        P("grp", "tile"),
        P("grp", "tile"),
        P(None, "tile"),
        P(None, "tile"),
    )
    return jax.shard_map(body, mesh=mesh, in_specs=in_specs, out_specs=P(None, "tile"), check_vma=False)
```

```python
import functools
import math

import jax
import jax.numpy as jnp
from jax import lax
from jax.experimental import pallas as pl
from jax.experimental.pallas import tpu as pltpu
from jax.sharding import PartitionSpec as P

SCANS_DEV = 64
TARGET_PTS = 512
LANES = 128
GROUP = 8
HALF = 32

DAMPING = 0.1
PRECISE = lax.Precision.HIGHEST
PAIRS = [(r, c) for r in range(6) for c in range(r, 6)]
PAIR_AT = {pair: at for at, pair in enumerate(PAIRS)}


def pack_kernel(
    dest_ref, scan_ref, points_ref, matches_ref, out_ref, slot_scan_ref, count_ref, slot_ref, *, capacity, blocks, points
):
    tiles = count_ref.shape[0]
    halves = points // LANES
    slots = tiles * capacity
    per_scan = blocks // SCANS_DEV
    out_ref[...] = jnp.full(out_ref.shape, -1.0, jnp.float32)

    def clear_count(at, carry):
        count_ref[at] = 0
        return carry

    def clear_slot(at, carry):
        slot_scan_ref[at] = -1
        return carry

    lax.fori_loop(0, tiles, clear_count, 0, unroll=8)
    lax.fori_loop(0, slots, clear_slot, 0, unroll=8)

    def rank(block, carry):
        dest = dest_ref[block]
        ranked = count_ref[dest]
        count_ref[dest] = ranked + 1
        slot = dest * capacity + ranked
        slot_scan_ref[slot] = block // per_scan
        slot_ref[block] = slot
        return carry

    lax.fori_loop(0, blocks, rank, 0, unroll=4)
    batch = 8

    def place(step, carry):
        loaded = []
        for at in range(batch):
            block = step * batch + at
            offset = scan_ref[block] * TARGET_PTS
            for half in range(halves):
                span = pl.ds(pl.multiple_of(block * points + half * LANES, LANES), LANES)
                wanted = matches_ref[:, span] + offset
                loaded.append((points_ref[0, :, span], wanted.astype(jnp.float32)))
        for at in range(batch):
            base = pl.multiple_of(slot_ref[step * batch + at] * (4 * halves), 8)
            for half in range(halves):
                coords, wanted = loaded[at * halves + half]
                out_ref[pl.ds(base + half * 4, 3), :] = coords
                out_ref[pl.ds(base + half * 4 + 3, 1), :] = wanted
        return carry

    lax.fori_loop(0, blocks // batch, place, 0)


def cross(first, second):
    return [
        first[1] * second[2] - first[2] * second[1],
        first[2] * second[0] - first[0] * second[2],
        first[0] * second[1] - first[1] * second[0],
    ]


def pair_kernel(x_ref, table_ref, own_ref, far_ref, owner_ref, all_ref, picked_ref, scan_ref, sem, *, points, fold):
    slots = far_ref.shape[0]
    groups = slots // GROUP
    halves = points // LANES
    chunks = TARGET_PTS // LANES
    lane = lax.broadcasted_iota(jnp.int32, (GROUP, LANES), 1)

    width = 4 * halves
    for at in range(slots // LANES):
        rows = x_ref[pl.ds(at * LANES * width + 3, LANES, stride=width), :]
        owner_ref[at : at + 1, :] = rows.T[0:1, :].astype(jnp.int32) >> 9
    copy = pltpu.make_async_copy(owner_ref, scan_ref, sem)
    copy.start()
    all_ref[...] = jnp.zeros(all_ref.shape, jnp.float32)
    copy.wait()

    def scan_at(item):
        return scan_ref[item // LANES, item % LANES]

    def maybe_group(group, carry):
        used = scan_at(group * GROUP)
        for item in range(1, GROUP):
            used = jnp.maximum(used, scan_at(group * GROUP + item))

        @pl.when(used >= 0)
        def _():
            one_group(group)

        return carry

    def one_group(group):
        base = pl.multiple_of(group * (4 * halves * GROUP), 8)

        def field(comp):
            parts = [x_ref[pl.ds(base + 4 * half + comp, GROUP, stride=4 * halves), :] for half in range(halves)]
            return jnp.concatenate(parts, axis=1)

        def chosen(comp):
            parts = [picked_ref[pl.ds(half * 8 * GROUP + comp, GROUP, stride=8), :] for half in range(halves)]
            return jnp.concatenate(parts, axis=1)

        index = field(3).astype(jnp.int32)
        valid = index >= 0
        low = index & (LANES - 1)
        high = (index >> 7) & (chunks - 1)
        for item in range(GROUP):
            scan = jnp.maximum(scan_at(group * GROUP + item), 0)
            start = pl.multiple_of(scan * TARGET_PTS, TARGET_PTS)
            parts = [
                table_ref[:, pl.ds(pl.multiple_of(start + at * LANES, LANES), LANES)] for at in range(chunks)
            ]
            for half in range(halves):
                span = slice(half * LANES, (half + 1) * LANES)
                low_at = jnp.broadcast_to(low[item : item + 1, span], (8, LANES))
                high_at = jnp.broadcast_to(high[item : item + 1, span], (8, LANES))
                found = jnp.take_along_axis(parts[0], low_at, axis=1, mode="promise_in_bounds")
                for at in range(1, chunks):
                    other = jnp.take_along_axis(parts[at], low_at, axis=1, mode="promise_in_bounds")
                    found = jnp.where(high_at == at, other, found)
                picked_ref[pl.ds((half * GROUP + item) * 8, 8), :] = found
        p = [field(comp) for comp in range(3)]
        q = [chosen(comp) for comp in range(3)]
        n = [jnp.where(valid, chosen(comp), 0.0) for comp in range(3, 6)]
        misfit = n[0] * (p[0] - q[0]) + n[1] * (p[1] - q[1]) + n[2] * (p[2] - q[2])
        own = cross(p, n) + n
        far = cross(q, n) + n

        def total(product):
            folded = product[:, :LANES]
            for half in range(1, halves):
                folded = folded + product[:, half * LANES : (half + 1) * LANES]
            return jnp.sum(folded, axis=1, keepdims=True)

        result = jnp.zeros((GROUP, LANES), jnp.float32)
        for at, (r, c) in enumerate(PAIRS):
            mine = total(own[r] * own[c])
            result = jnp.where(lane == at, mine, result)
            theirs = mine if r >= 3 else total(far[r] * far[c])
            result = jnp.where(lane == HALF + at, theirs, result)
        for at in range(6):
            mine = total(own[at] * misfit)
            result = jnp.where(lane == 21 + at, mine, result)
            theirs = mine if at >= 3 else total(far[at] * misfit)
            result = jnp.where(lane == HALF + 21 + at, -theirs, result)
        all_ref[pl.ds(pl.multiple_of(group * GROUP, GROUP), GROUP), :] = result

    lax.fori_loop(0, groups, maybe_group, 0)
    far_ref[...] = all_ref[...]
    rows = slots // fold
    wide = lax.broadcasted_iota(jnp.int32, (rows, LANES), 1) // HALF
    folded = all_ref[pl.ds(0, rows, stride=fold), :]
    for at in range(1, fold):
        moved = pltpu.roll(all_ref[pl.ds(at, rows, stride=fold), :], HALF * at, 1)
        folded = jnp.where(wide == at, moved, folded)
    own_ref[...] = folded


def solve_poses(totals):
    entries = [[totals[PAIR_AT[min(r, c), max(r, c)]] for c in range(6)] for r in range(6)]
    traced = entries[0][0]
    for at in range(1, 6):
        traced = traced + entries[at][at]
    shift_by = DAMPING * traced / 6.0
    for at in range(6):
        entries[at][at] = entries[at][at] + shift_by
    values = [-totals[21 + at] for at in range(6)]
    for pivot in range(6):
        for row in range(pivot + 1, 6):
            factor = entries[row][pivot] / entries[pivot][pivot]
            for col in range(pivot, 6):
                entries[row][col] = entries[row][col] - factor * entries[pivot][col]
            values[row] = values[row] - factor * values[pivot]
    result = [None] * 6
    for row in range(5, -1, -1):
        running = values[row]
        for col in range(row + 1, 6):
            running = running - entries[row][col] * result[col]
        result[row] = running / entries[row][row]
    return jnp.stack(result)


def body(source_points, intersection, target_scan, matches, target_points, target_normals):
    tiles = lax.axis_size("tile")
    blocks = intersection.shape[1]
    capacity = 2 * blocks // tiles
    slots = tiles * capacity
    points = source_points.shape[2] // blocks
    vmem = pl.BlockSpec(memory_space=pltpu.VMEM)
    smem = pl.BlockSpec(memory_space=pltpu.SMEM)
    message, slot_scan = pl.pallas_call(
        functools.partial(pack_kernel, capacity=capacity, blocks=blocks, points=points),
        out_shape=(
            jax.ShapeDtypeStruct((slots * 4 * points // LANES, LANES), jnp.float32),
            jax.ShapeDtypeStruct((slots,), jnp.int32),
        ),
        in_specs=[smem, smem, vmem, vmem],
        out_specs=(vmem, smem),
        scratch_shapes=[pltpu.SMEM((tiles,), jnp.int32), pltpu.SMEM((blocks,), jnp.int32)],
        name="pack",
    )(intersection.reshape(blocks), target_scan.reshape(blocks), source_points, matches)
    incoming = lax.all_to_all(message, "tile", split_axis=0, concat_axis=0, tiled=True)
    pad = jnp.zeros((2, target_points.shape[1]), jnp.float32)
    tables = jnp.concatenate([target_points, target_normals, pad], axis=0)
    fold = math.gcd(LANES // HALF, capacity)
    mine, terms, owner_scan = pl.pallas_call(
        functools.partial(pair_kernel, points=points, fold=fold),
        out_shape=(
            jax.ShapeDtypeStruct((slots // fold, LANES), jnp.float32),
            jax.ShapeDtypeStruct((slots, LANES), jnp.float32),
            jax.ShapeDtypeStruct((slots // LANES, LANES), jnp.int32),
        ),
        in_specs=[vmem, vmem],
        out_specs=(vmem, vmem, vmem),
        scratch_shapes=[
            pltpu.VMEM((slots, LANES), jnp.float32),
            pltpu.VMEM((GROUP * 8 * points // LANES, LANES), jnp.float32),
            pltpu.SMEM((slots // LANES, LANES), jnp.int32),
            pltpu.SemaphoreType.DMA,
        ],
        name="pairs",
    )(incoming, tables)
    returned = lax.all_to_all(mine, "tile", split_axis=0, concat_axis=0, tiled=True)
    scans = jnp.arange(SCANS_DEV, dtype=jnp.int32)
    tgt_onehot = (owner_scan.reshape(slots)[:, None] == scans[None, :]).astype(jnp.float32)
    contract = (((0,), (0,)), ((), ()))
    sums = lax.dot_general(terms[:, HALF : 2 * HALF], tgt_onehot, contract, precision=PRECISE)
    places = slot_scan.reshape(slots // fold, fold)
    for at in range(fold):
        src_onehot = (places[:, at][:, None] == scans[None, :]).astype(jnp.float32)
        part = returned[:, at * HALF : (at + 1) * HALF]
        sums = sums + lax.dot_general(part, src_onehot, contract, precision=PRECISE)
    totals = lax.psum(sums, "grp")
    return solve_poses(totals)


def solution(mesh):
    in_specs = (
        P("grp", None, "tile"),
        P("grp", "tile", None),
        P("grp", "tile"),
        P("grp", "tile"),
        P(None, "tile"),
        P(None, "tile"),
    )
    return jax.shard_map(body, mesh=mesh, in_specs=in_specs, out_specs=P(None, "tile"), check_vma=False)
```

```python
import functools
import math

import jax
import jax.numpy as jnp
from jax import lax
from jax.experimental import pallas as pl
from jax.experimental.pallas import tpu as pltpu
from jax.sharding import PartitionSpec as P

SCANS_DEV = 64
TARGET_PTS = 512
LANES = 128
GROUP = 8
HALF = 32
WAVES = 4

DAMPING = 0.1
PRECISE = lax.Precision.HIGHEST
PAIRS = [(r, c) for r in range(6) for c in range(r, 6)]
PAIR_AT = {pair: at for at, pair in enumerate(PAIRS)}


def pack_kernel(
    me_ref, dest_ref, scan_ref, points_ref, matches_ref, *refs, capacity, blocks, points
):
    slot_scan_ref, out_ref, count_ref, slot_ref = refs[-4:]
    chunk_refs = refs[:-4]
    me = me_ref[0]
    tiles = count_ref.shape[0]
    halves = points // LANES
    slots = tiles * capacity
    per_scan = blocks // SCANS_DEV
    out_ref[...] = jnp.full(out_ref.shape, -1.0, jnp.float32)

    def clear_count(at, carry):
        count_ref[at] = 0
        return carry

    def clear_slot(at, carry):
        slot_scan_ref[at] = -1
        return carry

    lax.fori_loop(0, tiles, clear_count, 0, unroll=8)
    lax.fori_loop(0, slots, clear_slot, 0, unroll=8)

    def rank(block, carry):
        dest = dest_ref[block]
        ranked = count_ref[dest]
        count_ref[dest] = ranked + 1
        ahead = dest - me
        slot = jnp.where(ahead < 0, ahead + tiles, ahead) * capacity + ranked
        slot_scan_ref[slot] = block // per_scan
        slot_ref[block] = slot
        return carry

    lax.fori_loop(0, blocks, rank, 0, unroll=4)
    batch = 8

    def place(step, carry):
        loaded = []
        for at in range(batch):
            block = step * batch + at
            offset = scan_ref[block] * TARGET_PTS
            for half in range(halves):
                span = pl.ds(pl.multiple_of(block * points + half * LANES, LANES), LANES)
                wanted = matches_ref[:, span] + offset
                loaded.append((points_ref[0, :, span], wanted.astype(jnp.float32)))
        for at in range(batch):
            base = pl.multiple_of(slot_ref[step * batch + at] * (4 * halves), 8)
            for half in range(halves):
                coords, wanted = loaded[at * halves + half]
                out_ref[pl.ds(base + half * 4, 3), :] = coords
                out_ref[pl.ds(base + half * 4 + 3, 1), :] = wanted
        return carry

    lax.fori_loop(0, blocks // batch, place, 0)
    for at, chunk_ref in enumerate(chunk_refs):
        rows = chunk_ref.shape[0]
        chunk_ref[...] = out_ref[at * rows : (at + 1) * rows, :]


def cross(first, second):
    return [
        first[1] * second[2] - first[2] * second[1],
        first[2] * second[0] - first[0] * second[2],
        first[0] * second[1] - first[1] * second[0],
    ]


def pair_kernel(table_ref, *refs, points, fold, chunks_in):
    sources = refs[:chunks_in]
    own_refs = refs[chunks_in : 2 * chunks_in]
    far_ref, owner_ref, x_ref, all_ref, picked_ref, scan_ref, sem = refs[2 * chunks_in :]
    slots = far_ref.shape[0]
    groups = slots // GROUP
    halves = points // LANES
    chunks = TARGET_PTS // LANES
    lane = lax.broadcasted_iota(jnp.int32, (GROUP, LANES), 1)

    width = 4 * halves
    step = owner_ref.shape[1]
    for at, source in enumerate(sources):
        rows = source.shape[0]
        x_ref[at * rows : (at + 1) * rows, :] = source[...]
    for at in range(slots // step):
        rows = x_ref[pl.ds(at * step * width + 3, step, stride=width), :]
        owner_ref[at : at + 1, :] = rows.T[0:1, :].astype(jnp.int32) >> 9
    copy = pltpu.make_async_copy(owner_ref, scan_ref, sem)
    copy.start()
    all_ref[...] = jnp.zeros(all_ref.shape, jnp.float32)
    copy.wait()

    def scan_at(item):
        return scan_ref[item // step, item % step]

    def maybe_group(group, carry):
        used = scan_at(group * GROUP)
        for item in range(1, GROUP):
            used = jnp.maximum(used, scan_at(group * GROUP + item))

        @pl.when(used >= 0)
        def _():
            one_group(group)

        return carry

    def one_group(group):
        base = pl.multiple_of(group * (4 * halves * GROUP), 8)

        def field(comp):
            parts = [x_ref[pl.ds(base + 4 * half + comp, GROUP, stride=4 * halves), :] for half in range(halves)]
            return jnp.concatenate(parts, axis=1)

        def chosen(comp):
            parts = [picked_ref[pl.ds(half * 8 * GROUP + comp, GROUP, stride=8), :] for half in range(halves)]
            return jnp.concatenate(parts, axis=1)

        index = field(3).astype(jnp.int32)
        valid = index >= 0
        low = index & (LANES - 1)
        high = (index >> 7) & (chunks - 1)
        for item in range(GROUP):
            scan = jnp.maximum(scan_at(group * GROUP + item), 0)
            start = pl.multiple_of(scan * TARGET_PTS, TARGET_PTS)
            parts = [
                table_ref[:, pl.ds(pl.multiple_of(start + at * LANES, LANES), LANES)] for at in range(chunks)
            ]
            for half in range(halves):
                span = slice(half * LANES, (half + 1) * LANES)
                low_at = jnp.broadcast_to(low[item : item + 1, span], (8, LANES))
                high_at = jnp.broadcast_to(high[item : item + 1, span], (8, LANES))
                found = jnp.take_along_axis(parts[0], low_at, axis=1, mode="promise_in_bounds")
                for at in range(1, chunks):
                    other = jnp.take_along_axis(parts[at], low_at, axis=1, mode="promise_in_bounds")
                    found = jnp.where(high_at == at, other, found)
                picked_ref[pl.ds((half * GROUP + item) * 8, 8), :] = found
        p = [field(comp) for comp in range(3)]
        q = [chosen(comp) for comp in range(3)]
        n = [jnp.where(valid, chosen(comp), 0.0) for comp in range(3, 6)]
        misfit = n[0] * (p[0] - q[0]) + n[1] * (p[1] - q[1]) + n[2] * (p[2] - q[2])
        own = cross(p, n) + n
        far = cross(q, n) + n

        def total(product):
            folded = product[:, :LANES]
            for half in range(1, halves):
                folded = folded + product[:, half * LANES : (half + 1) * LANES]
            return jnp.sum(folded, axis=1, keepdims=True)

        result = jnp.zeros((GROUP, LANES), jnp.float32)
        for at, (r, c) in enumerate(PAIRS):
            mine = total(own[r] * own[c])
            result = jnp.where(lane == at, mine, result)
            theirs = mine if r >= 3 else total(far[r] * far[c])
            result = jnp.where(lane == HALF + at, theirs, result)
        for at in range(6):
            mine = total(own[at] * misfit)
            result = jnp.where(lane == 21 + at, mine, result)
            theirs = mine if at >= 3 else total(far[at] * misfit)
            result = jnp.where(lane == HALF + 21 + at, -theirs, result)
        all_ref[pl.ds(pl.multiple_of(group * GROUP, GROUP), GROUP), :] = result

    lax.fori_loop(0, groups, maybe_group, 0)
    far_ref[...] = all_ref[...]
    rows = slots // fold
    wide = lax.broadcasted_iota(jnp.int32, (rows, LANES), 1) // HALF
    folded = all_ref[pl.ds(0, rows, stride=fold), :]
    for at in range(1, fold):
        moved = pltpu.roll(all_ref[pl.ds(at, rows, stride=fold), :], HALF * at, 1)
        folded = jnp.where(wide == at, moved, folded)
    for at, own_ref in enumerate(own_refs):
        rows = own_ref.shape[0]
        own_ref[...] = folded[at * rows : (at + 1) * rows, :]


def solve_poses(totals):
    entries = [[totals[PAIR_AT[min(r, c), max(r, c)]] for c in range(6)] for r in range(6)]
    traced = entries[0][0]
    for at in range(1, 6):
        traced = traced + entries[at][at]
    shift_by = DAMPING * traced / 6.0
    for at in range(6):
        entries[at][at] = entries[at][at] + shift_by
    values = [-totals[21 + at] for at in range(6)]
    for pivot in range(6):
        for row in range(pivot + 1, 6):
            factor = entries[row][pivot] / entries[pivot][pivot]
            for col in range(pivot, 6):
                entries[row][col] = entries[row][col] - factor * entries[pivot][col]
            values[row] = values[row] - factor * values[pivot]
    result = [None] * 6
    for row in range(5, -1, -1):
        running = values[row]
        for col in range(row + 1, 6):
            running = running - entries[row][col] * result[col]
        result[row] = running / entries[row][row]
    return jnp.stack(result)


def body(source_points, intersection, target_scan, matches, target_points, target_normals):
    tiles = lax.axis_size("tile")
    blocks = intersection.shape[1]
    capacity = 2 * blocks // tiles
    slots = tiles * capacity
    points = source_points.shape[2] // blocks
    vmem = pl.BlockSpec(memory_space=pltpu.VMEM)
    smem = pl.BlockSpec(memory_space=pltpu.SMEM)
    whole_rows = slots * 4 * points // LANES
    chunk_shape = jax.ShapeDtypeStruct((whole_rows // tiles, LANES), jnp.float32)
    me = lax.axis_index("tile").astype(jnp.int32).reshape(1)
    *chunks, slot_scan = pl.pallas_call(
        functools.partial(pack_kernel, capacity=capacity, blocks=blocks, points=points),
        out_shape=(chunk_shape,) * tiles + (jax.ShapeDtypeStruct((slots,), jnp.int32),),
        in_specs=[smem, smem, smem, vmem, vmem],
        out_specs=(vmem,) * tiles + (smem,),
        scratch_shapes=[
            pltpu.VMEM((whole_rows, LANES), jnp.float32),
            pltpu.SMEM((tiles,), jnp.int32),
            pltpu.SMEM((blocks,), jnp.int32),
        ],
        name="pack",
    )(me, intersection.reshape(blocks), target_scan.reshape(blocks), source_points, matches)

    def shift(array, ahead):
        if ahead % tiles == 0:
            return array
        return lax.ppermute(array, "tile", [(i, (i + ahead) % tiles) for i in range(tiles)])

    incoming = [shift(chunk, ahead) for ahead, chunk in enumerate(chunks)]
    pad = jnp.zeros((2, target_points.shape[1]), jnp.float32)
    tables = jnp.concatenate([target_points, target_normals, pad], axis=0)
    fold = math.gcd(LANES // HALF, capacity)
    group_count = math.gcd(tiles, WAVES)
    per_group = tiles // group_count
    part = per_group * capacity
    step = math.gcd(part, LANES)
    own_shape = jax.ShapeDtypeStruct((capacity // fold, LANES), jnp.float32)
    mine, terms, owners = [], [], []
    for at in range(group_count):
        *own_parts, far_part, owner_part = pl.pallas_call(
            functools.partial(pair_kernel, points=points, fold=fold, chunks_in=per_group),
            out_shape=(own_shape,) * per_group
            + (
                jax.ShapeDtypeStruct((part, LANES), jnp.float32),
                jax.ShapeDtypeStruct((part // step, step), jnp.int32),
            ),
            in_specs=[vmem] * (per_group + 1),
            out_specs=(vmem,) * (per_group + 2),
            scratch_shapes=[
                pltpu.VMEM((part * 4 * points // LANES, LANES), jnp.float32),
                pltpu.VMEM((part, LANES), jnp.float32),
                pltpu.VMEM((GROUP * 8 * points // LANES, LANES), jnp.float32),
                pltpu.SMEM((part // step, step), jnp.int32),
                pltpu.SemaphoreType.DMA,
            ],
            name="pairs",
        )(tables, *incoming[at * per_group : (at + 1) * per_group])
        mine.extend(own_parts)
        terms.append(far_part)
        owners.append(owner_part.reshape(part))
    terms = jnp.concatenate(terms, axis=0)
    owner_scan = jnp.concatenate(owners, axis=0)
    returned = jnp.concatenate([shift(chunk, -ahead) for ahead, chunk in enumerate(mine)], axis=0)
    scans = jnp.arange(SCANS_DEV, dtype=jnp.int32)
    tgt_onehot = (owner_scan.reshape(slots)[:, None] == scans[None, :]).astype(jnp.float32)
    contract = (((0,), (0,)), ((), ()))
    sums = lax.dot_general(terms[:, HALF : 2 * HALF], tgt_onehot, contract, precision=PRECISE)
    places = slot_scan.reshape(slots // fold, fold)
    for at in range(fold):
        src_onehot = (places[:, at][:, None] == scans[None, :]).astype(jnp.float32)
        part = returned[:, at * HALF : (at + 1) * HALF]
        sums = sums + lax.dot_general(part, src_onehot, contract, precision=PRECISE)
    totals = lax.psum(sums, "grp")
    return solve_poses(totals)


def solution(mesh):
    in_specs = (
        P("grp", None, "tile"),
        P("grp", "tile", None),
        P("grp", "tile"),
        P("grp", "tile"),
        P(None, "tile"),
        P(None, "tile"),
    )
    return jax.shard_map(body, mesh=mesh, in_specs=in_specs, out_specs=P(None, "tile"), check_vma=False)
```

```python
import functools
import math

import jax
import jax.numpy as jnp
from jax import lax
from jax.experimental import pallas as pl
from jax.experimental.pallas import tpu as pltpu
from jax.sharding import PartitionSpec as P

SCANS_DEV = 64
TARGET_PTS = 512
LANES = 128
GROUP = 8
HALF = 32

DAMPING = 0.1
PRECISE = lax.Precision.HIGHEST
PAIRS = [(r, c) for r in range(6) for c in range(r, 6)]
PAIR_AT = {pair: at for at, pair in enumerate(PAIRS)}


def pack_kernel(
    me_ref, dest_ref, scan_ref, points_ref, matches_ref, *refs, capacity, blocks, points
):
    slot_scan_ref, out_ref, count_ref, slot_ref = refs[-4:]
    chunk_refs = refs[:-4]
    me = me_ref[0]
    tiles = count_ref.shape[0]
    halves = points // LANES
    slots = tiles * capacity
    per_scan = blocks // SCANS_DEV
    out_ref[...] = jnp.full(out_ref.shape, -1.0, jnp.float32)

    def clear_count(at, carry):
        count_ref[at] = 0
        return carry

    def clear_slot(at, carry):
        slot_scan_ref[at] = -1
        return carry

    lax.fori_loop(0, tiles, clear_count, 0, unroll=8)
    lax.fori_loop(0, slots, clear_slot, 0, unroll=8)

    def rank(block, carry):
        dest = dest_ref[block]
        ranked = count_ref[dest]
        count_ref[dest] = ranked + 1
        ahead = dest - me
        slot = jnp.where(ahead < 0, ahead + tiles, ahead) * capacity + ranked
        slot_scan_ref[dest * capacity + ranked] = block // per_scan
        slot_ref[block] = slot
        return carry

    lax.fori_loop(0, blocks, rank, 0, unroll=4)
    batch = 8

    def place(step, carry):
        loaded = []
        for at in range(batch):
            block = step * batch + at
            offset = scan_ref[block] * TARGET_PTS
            for half in range(halves):
                span = pl.ds(pl.multiple_of(block * points + half * LANES, LANES), LANES)
                wanted = matches_ref[:, span] + offset
                loaded.append((points_ref[0, :, span], wanted.astype(jnp.float32)))
        for at in range(batch):
            base = pl.multiple_of(slot_ref[step * batch + at] * (4 * halves), 8)
            for half in range(halves):
                coords, wanted = loaded[at * halves + half]
                out_ref[pl.ds(base + half * 4, 3), :] = coords
                out_ref[pl.ds(base + half * 4 + 3, 1), :] = wanted
        return carry

    lax.fori_loop(0, blocks // batch, place, 0)
    for at, chunk_ref in enumerate(chunk_refs):
        rows = chunk_ref.shape[0]
        chunk_ref[...] = out_ref[at * rows : (at + 1) * rows, :]


def cross(first, second):
    return [
        first[1] * second[2] - first[2] * second[1],
        first[2] * second[0] - first[0] * second[2],
        first[0] * second[1] - first[1] * second[0],
    ]


def pair_kernel(me_ref, table_ref, *refs, points, fold, chunks_in):
    sources = refs[:chunks_in]
    own_ref, far_ref, owner_ref, x_ref, all_ref, picked_ref, scan_ref, sem = refs[chunks_in:]
    slots = far_ref.shape[0]
    groups = slots // GROUP
    halves = points // LANES
    chunks = TARGET_PTS // LANES
    lane = lax.broadcasted_iota(jnp.int32, (GROUP, LANES), 1)

    width = 4 * halves
    step = owner_ref.shape[1]
    for at, source in enumerate(sources):
        rows = source.shape[0]
        x_ref[at * rows : (at + 1) * rows, :] = source[...]
    for at in range(slots // step):
        rows = x_ref[pl.ds(at * step * width + 3, step, stride=width), :]
        owner_ref[at : at + 1, :] = rows.T[0:1, :].astype(jnp.int32) >> 9
    copy = pltpu.make_async_copy(owner_ref, scan_ref, sem)
    copy.start()
    all_ref[...] = jnp.zeros(all_ref.shape, jnp.float32)
    copy.wait()

    def scan_at(item):
        return scan_ref[item // step, item % step]

    def maybe_group(group, carry):
        used = scan_at(group * GROUP)
        for item in range(1, GROUP):
            used = jnp.maximum(used, scan_at(group * GROUP + item))

        @pl.when(used >= 0)
        def _():
            one_group(group)

        return carry

    def one_group(group):
        base = pl.multiple_of(group * (4 * halves * GROUP), 8)

        def field(comp):
            parts = [x_ref[pl.ds(base + 4 * half + comp, GROUP, stride=4 * halves), :] for half in range(halves)]
            return jnp.concatenate(parts, axis=1)

        def chosen(comp):
            parts = [picked_ref[pl.ds(half * 8 * GROUP + comp, GROUP, stride=8), :] for half in range(halves)]
            return jnp.concatenate(parts, axis=1)

        index = field(3).astype(jnp.int32)
        valid = index >= 0
        low = index & (LANES - 1)
        high = (index >> 7) & (chunks - 1)
        for item in range(GROUP):
            scan = jnp.maximum(scan_at(group * GROUP + item), 0)
            start = pl.multiple_of(scan * TARGET_PTS, TARGET_PTS)
            parts = [
                table_ref[:, pl.ds(pl.multiple_of(start + at * LANES, LANES), LANES)] for at in range(chunks)
            ]
            for half in range(halves):
                span = slice(half * LANES, (half + 1) * LANES)
                low_at = jnp.broadcast_to(low[item : item + 1, span], (8, LANES))
                high_at = jnp.broadcast_to(high[item : item + 1, span], (8, LANES))
                found = jnp.take_along_axis(parts[0], low_at, axis=1, mode="promise_in_bounds")
                for at in range(1, chunks):
                    other = jnp.take_along_axis(parts[at], low_at, axis=1, mode="promise_in_bounds")
                    found = jnp.where(high_at == at, other, found)
                picked_ref[pl.ds((half * GROUP + item) * 8, 8), :] = found
        p = [field(comp) for comp in range(3)]
        q = [chosen(comp) for comp in range(3)]
        n = [jnp.where(valid, chosen(comp), 0.0) for comp in range(3, 6)]
        misfit = n[0] * (p[0] - q[0]) + n[1] * (p[1] - q[1]) + n[2] * (p[2] - q[2])
        own = cross(p, n) + n
        far = cross(q, n) + n

        def total(product):
            folded = product[:, :LANES]
            for half in range(1, halves):
                folded = folded + product[:, half * LANES : (half + 1) * LANES]
            return jnp.sum(folded, axis=1, keepdims=True)

        result = jnp.zeros((GROUP, LANES), jnp.float32)
        for at, (r, c) in enumerate(PAIRS):
            mine = total(own[r] * own[c])
            result = jnp.where(lane == at, mine, result)
            theirs = mine if r >= 3 else total(far[r] * far[c])
            result = jnp.where(lane == HALF + at, theirs, result)
        for at in range(6):
            mine = total(own[at] * misfit)
            result = jnp.where(lane == 21 + at, mine, result)
            theirs = mine if at >= 3 else total(far[at] * misfit)
            result = jnp.where(lane == HALF + 21 + at, -theirs, result)
        all_ref[pl.ds(pl.multiple_of(group * GROUP, GROUP), GROUP), :] = result

    lax.fori_loop(0, groups, maybe_group, 0)
    far_ref[...] = all_ref[...]
    rows = slots // fold
    wide = lax.broadcasted_iota(jnp.int32, (rows, LANES), 1) // HALF
    folded = all_ref[pl.ds(0, rows, stride=fold), :]
    for at in range(1, fold):
        moved = pltpu.roll(all_ref[pl.ds(at, rows, stride=fold), :], HALF * at, 1)
        folded = jnp.where(wide == at, moved, folded)
    chunk = rows // chunks_in
    for at in range(chunks_in):
        back = me_ref[0] - at
        place = jnp.where(back < 0, back + chunks_in, back) * chunk
        own_ref[pl.ds(place, chunk), :] = folded[at * chunk : (at + 1) * chunk, :]


def solve_poses(totals):
    entries = [[totals[PAIR_AT[min(r, c), max(r, c)]] for c in range(6)] for r in range(6)]
    traced = entries[0][0]
    for at in range(1, 6):
        traced = traced + entries[at][at]
    shift_by = DAMPING * traced / 6.0
    for at in range(6):
        entries[at][at] = entries[at][at] + shift_by
    values = [-totals[21 + at] for at in range(6)]
    for pivot in range(6):
        for row in range(pivot + 1, 6):
            factor = entries[row][pivot] / entries[pivot][pivot]
            for col in range(pivot, 6):
                entries[row][col] = entries[row][col] - factor * entries[pivot][col]
            values[row] = values[row] - factor * values[pivot]
    result = [None] * 6
    for row in range(5, -1, -1):
        running = values[row]
        for col in range(row + 1, 6):
            running = running - entries[row][col] * result[col]
        result[row] = running / entries[row][row]
    return jnp.stack(result)


def body(source_points, intersection, target_scan, matches, target_points, target_normals):
    tiles = lax.axis_size("tile")
    blocks = intersection.shape[1]
    capacity = 2 * blocks // tiles
    slots = tiles * capacity
    points = source_points.shape[2] // blocks
    vmem = pl.BlockSpec(memory_space=pltpu.VMEM)
    smem = pl.BlockSpec(memory_space=pltpu.SMEM)
    whole_rows = slots * 4 * points // LANES
    chunk_shape = jax.ShapeDtypeStruct((whole_rows // tiles, LANES), jnp.float32)
    me = lax.axis_index("tile").astype(jnp.int32).reshape(1)
    *chunks, slot_scan = pl.pallas_call(
        functools.partial(pack_kernel, capacity=capacity, blocks=blocks, points=points),
        out_shape=(chunk_shape,) * tiles + (jax.ShapeDtypeStruct((slots,), jnp.int32),),
        in_specs=[smem, smem, smem, vmem, vmem],
        out_specs=(vmem,) * tiles + (smem,),
        scratch_shapes=[
            pltpu.VMEM((whole_rows, LANES), jnp.float32),
            pltpu.SMEM((tiles,), jnp.int32),
            pltpu.SMEM((blocks,), jnp.int32),
        ],
        name="pack",
    )(me, intersection.reshape(blocks), target_scan.reshape(blocks), source_points, matches)

    def shift(array, ahead):
        if ahead % tiles == 0:
            return array
        return lax.ppermute(array, "tile", [(i, (i + ahead) % tiles) for i in range(tiles)])

    incoming = [shift(chunk, ahead) for ahead, chunk in enumerate(chunks)]
    pad = jnp.zeros((2, target_points.shape[1]), jnp.float32)
    tables = jnp.concatenate([target_points, target_normals, pad], axis=0)
    fold = math.gcd(LANES // HALF, capacity)
    step = math.gcd(slots, LANES)
    mine, terms, owner_scan = pl.pallas_call(
        functools.partial(pair_kernel, points=points, fold=fold, chunks_in=tiles),
        out_shape=(
            jax.ShapeDtypeStruct((slots // fold, LANES), jnp.float32),
            jax.ShapeDtypeStruct((slots, LANES), jnp.float32),
            jax.ShapeDtypeStruct((slots // step, step), jnp.int32),
        ),
        in_specs=[smem] + [vmem] * (tiles + 1),
        out_specs=(vmem,) * 3,
        scratch_shapes=[
            pltpu.VMEM((whole_rows, LANES), jnp.float32),
            pltpu.VMEM((slots, LANES), jnp.float32),
            pltpu.VMEM((GROUP * 8 * points // LANES, LANES), jnp.float32),
            pltpu.SMEM((slots // step, step), jnp.int32),
            pltpu.SemaphoreType.DMA,
        ],
        name="pairs",
    )(me, tables, *incoming)
    owner_scan = owner_scan.reshape(slots)
    returned = lax.all_to_all(mine, "tile", split_axis=0, concat_axis=0, tiled=True)
    scans = jnp.arange(SCANS_DEV, dtype=jnp.int32)
    tgt_onehot = (owner_scan[:, None] == scans[None, :]).astype(jnp.float32)
    contract = (((0,), (0,)), ((), ()))
    sums = lax.dot_general(terms[:, HALF : 2 * HALF], tgt_onehot, contract, precision=PRECISE)
    places = slot_scan.reshape(slots // fold, fold)
    for at in range(fold):
        src_onehot = (places[:, at][:, None] == scans[None, :]).astype(jnp.float32)
        part = returned[:, at * HALF : (at + 1) * HALF]
        sums = sums + lax.dot_general(part, src_onehot, contract, precision=PRECISE)
    totals = lax.psum(sums, "grp")
    return solve_poses(totals)


def solution(mesh):
    in_specs = (
        P("grp", None, "tile"),
        P("grp", "tile", None),
        P("grp", "tile"),
        P("grp", "tile"),
        P(None, "tile"),
        P(None, "tile"),
    )
    return jax.shard_map(body, mesh=mesh, in_specs=in_specs, out_specs=P(None, "tile"), check_vma=False)
```

```python
import functools
import math

import jax
import jax.numpy as jnp
from jax import lax
from jax.experimental import pallas as pl
from jax.experimental.pallas import tpu as pltpu
from jax.sharding import PartitionSpec as P

SCANS_DEV = 64
TARGET_PTS = 512
LANES = 128
GROUP = 8
HALF = 32

DAMPING = 0.1
PRECISE = lax.Precision.HIGHEST
PAIRS = [(r, c) for r in range(6) for c in range(r, 6)]
PAIR_AT = {pair: at for at, pair in enumerate(PAIRS)}


def pack_kernel(
    dest_ref, scan_ref, points_ref, matches_ref, out_ref, slot_scan_ref, count_ref, slot_ref, *, capacity, blocks, points
):
    tiles = count_ref.shape[0]
    halves = points // LANES
    slots = tiles * capacity
    per_scan = blocks // SCANS_DEV
    out_ref[...] = jnp.full(out_ref.shape, -1.0, jnp.float32)

    def clear_count(at, carry):
        count_ref[at] = 0
        return carry

    def clear_slot(at, carry):
        slot_scan_ref[at] = -1
        return carry

    lax.fori_loop(0, tiles, clear_count, 0, unroll=8)
    lax.fori_loop(0, slots, clear_slot, 0, unroll=8)

    def rank(block, carry):
        dest = dest_ref[block]
        ranked = count_ref[dest]
        count_ref[dest] = ranked + 1
        slot = dest * capacity + ranked
        slot_scan_ref[slot] = block // per_scan
        slot_ref[block] = slot
        return carry

    lax.fori_loop(0, blocks, rank, 0, unroll=4)
    batch = 8

    def place(step, carry):
        loaded = []
        for at in range(batch):
            block = step * batch + at
            offset = scan_ref[block] * TARGET_PTS
            for half in range(halves):
                span = pl.ds(pl.multiple_of(block * points + half * LANES, LANES), LANES)
                wanted = matches_ref[:, span] + offset
                loaded.append((points_ref[0, :, span], wanted.astype(jnp.float32)))
        for at in range(batch):
            base = pl.multiple_of(slot_ref[step * batch + at] * (4 * halves), 8)
            for half in range(halves):
                coords, wanted = loaded[at * halves + half]
                out_ref[pl.ds(base + half * 4, 3), :] = coords
                out_ref[pl.ds(base + half * 4 + 3, 1), :] = wanted
        return carry

    lax.fori_loop(0, blocks // batch, place, 0)


def cross(first, second):
    return [
        first[1] * second[2] - first[2] * second[1],
        first[2] * second[0] - first[0] * second[2],
        first[0] * second[1] - first[1] * second[0],
    ]


def pair_kernel(x_ref, table_ref, own_ref, far_ref, owner_ref, all_ref, picked_ref, scan_ref, list_ref, sem, *, points, fold):
    slots = far_ref.shape[0]
    groups = slots // GROUP
    halves = points // LANES
    chunks = TARGET_PTS // LANES
    lane = lax.broadcasted_iota(jnp.int32, (GROUP, LANES), 1)

    width = 4 * halves
    for at in range(slots // LANES):
        rows = x_ref[pl.ds(at * LANES * width + 3, LANES, stride=width), :]
        owner_ref[at : at + 1, :] = rows.T[0:1, :].astype(jnp.int32) >> 9
    copy = pltpu.make_async_copy(owner_ref, scan_ref, sem)
    copy.start()
    all_ref[...] = jnp.zeros(all_ref.shape, jnp.float32)
    copy.wait()

    def scan_at(item):
        return scan_ref[item // LANES, item % LANES]

    def list_group(group, count):
        used = scan_at(group * GROUP)
        for item in range(1, GROUP):
            used = jnp.maximum(used, scan_at(group * GROUP + item))
        list_ref[count] = group
        list_ref[count + 1] = group
        return count + jnp.where(used >= 0, 1, 0)

    def one_group(group, lane_of):
        picked_at = lane_of * halves * 8 * GROUP
        base = pl.multiple_of(group * (4 * halves * GROUP), 8)

        def field(comp):
            parts = [x_ref[pl.ds(base + 4 * half + comp, GROUP, stride=4 * halves), :] for half in range(halves)]
            return jnp.concatenate(parts, axis=1)

        def chosen(comp):
            parts = [picked_ref[pl.ds(picked_at + half * 8 * GROUP + comp, GROUP, stride=8), :] for half in range(halves)]
            return jnp.concatenate(parts, axis=1)

        index = field(3).astype(jnp.int32)
        valid = index >= 0
        low = index & (LANES - 1)
        high = (index >> 7) & (chunks - 1)
        for item in range(GROUP):
            scan = jnp.maximum(scan_at(group * GROUP + item), 0)
            start = pl.multiple_of(scan * TARGET_PTS, TARGET_PTS)
            parts = [
                table_ref[:, pl.ds(pl.multiple_of(start + at * LANES, LANES), LANES)] for at in range(chunks)
            ]
            for half in range(halves):
                span = slice(half * LANES, (half + 1) * LANES)
                low_at = jnp.broadcast_to(low[item : item + 1, span], (8, LANES))
                high_at = jnp.broadcast_to(high[item : item + 1, span], (8, LANES))
                found = jnp.take_along_axis(parts[0], low_at, axis=1, mode="promise_in_bounds")
                for at in range(1, chunks):
                    other = jnp.take_along_axis(parts[at], low_at, axis=1, mode="promise_in_bounds")
                    found = jnp.where(high_at == at, other, found)
                picked_ref[pl.ds(picked_at + (half * GROUP + item) * 8, 8), :] = found
        p = [field(comp) for comp in range(3)]
        q = [chosen(comp) for comp in range(3)]
        n = [jnp.where(valid, chosen(comp), 0.0) for comp in range(3, 6)]
        misfit = n[0] * (p[0] - q[0]) + n[1] * (p[1] - q[1]) + n[2] * (p[2] - q[2])
        own = cross(p, n) + n
        far = cross(q, n) + n

        def total(product):
            folded = product[:, :LANES]
            for half in range(1, halves):
                folded = folded + product[:, half * LANES : (half + 1) * LANES]
            return jnp.sum(folded, axis=1, keepdims=True)

        result = jnp.zeros((GROUP, LANES), jnp.float32)
        for at, (r, c) in enumerate(PAIRS):
            mine = total(own[r] * own[c])
            result = jnp.where(lane == at, mine, result)
            theirs = mine if r >= 3 else total(far[r] * far[c])
            result = jnp.where(lane == HALF + at, theirs, result)
        for at in range(6):
            mine = total(own[at] * misfit)
            result = jnp.where(lane == 21 + at, mine, result)
            theirs = mine if at >= 3 else total(far[at] * misfit)
            result = jnp.where(lane == HALF + 21 + at, -theirs, result)
        return result

    def two_groups(at, carry):
        pair = [list_ref[2 * at], list_ref[jnp.minimum(2 * at + 1, count - 1)]]
        results = [one_group(group, lane_of) for lane_of, group in enumerate(pair)]
        for group, result in zip(pair, results):
            all_ref[pl.ds(pl.multiple_of(group * GROUP, GROUP), GROUP), :] = result
        return carry

    count = lax.fori_loop(0, groups, list_group, 0)
    lax.fori_loop(0, (count + 1) // 2, two_groups, 0)
    far_ref[...] = all_ref[...]
    rows = slots // fold
    wide = lax.broadcasted_iota(jnp.int32, (rows, LANES), 1) // HALF
    folded = all_ref[pl.ds(0, rows, stride=fold), :]
    for at in range(1, fold):
        moved = pltpu.roll(all_ref[pl.ds(at, rows, stride=fold), :], HALF * at, 1)
        folded = jnp.where(wide == at, moved, folded)
    own_ref[...] = folded


def solve_poses(totals):
    entries = [[totals[PAIR_AT[min(r, c), max(r, c)]] for c in range(6)] for r in range(6)]
    traced = entries[0][0]
    for at in range(1, 6):
        traced = traced + entries[at][at]
    shift_by = DAMPING * traced / 6.0
    for at in range(6):
        entries[at][at] = entries[at][at] + shift_by
    values = [-totals[21 + at] for at in range(6)]
    for pivot in range(6):
        for row in range(pivot + 1, 6):
            factor = entries[row][pivot] / entries[pivot][pivot]
            for col in range(pivot, 6):
                entries[row][col] = entries[row][col] - factor * entries[pivot][col]
            values[row] = values[row] - factor * values[pivot]
    result = [None] * 6
    for row in range(5, -1, -1):
        running = values[row]
        for col in range(row + 1, 6):
            running = running - entries[row][col] * result[col]
        result[row] = running / entries[row][row]
    return jnp.stack(result)


def body(source_points, intersection, target_scan, matches, target_points, target_normals):
    tiles = lax.axis_size("tile")
    blocks = intersection.shape[1]
    capacity = 2 * blocks // tiles
    slots = tiles * capacity
    points = source_points.shape[2] // blocks
    vmem = pl.BlockSpec(memory_space=pltpu.VMEM)
    smem = pl.BlockSpec(memory_space=pltpu.SMEM)
    message, slot_scan = pl.pallas_call(
        functools.partial(pack_kernel, capacity=capacity, blocks=blocks, points=points),
        out_shape=(
            jax.ShapeDtypeStruct((slots * 4 * points // LANES, LANES), jnp.float32),
            jax.ShapeDtypeStruct((slots,), jnp.int32),
        ),
        in_specs=[smem, smem, vmem, vmem],
        out_specs=(vmem, smem),
        scratch_shapes=[pltpu.SMEM((tiles,), jnp.int32), pltpu.SMEM((blocks,), jnp.int32)],
        name="pack",
    )(intersection.reshape(blocks), target_scan.reshape(blocks), source_points, matches)
    incoming = lax.all_to_all(message, "tile", split_axis=0, concat_axis=0, tiled=True)
    pad = jnp.zeros((2, target_points.shape[1]), jnp.float32)
    tables = jnp.concatenate([target_points, target_normals, pad], axis=0)
    fold = math.gcd(LANES // HALF, capacity)
    mine, terms, owner_scan = pl.pallas_call(
        functools.partial(pair_kernel, points=points, fold=fold),
        out_shape=(
            jax.ShapeDtypeStruct((slots // fold, LANES), jnp.float32),
            jax.ShapeDtypeStruct((slots, LANES), jnp.float32),
            jax.ShapeDtypeStruct((slots // LANES, LANES), jnp.int32),
        ),
        in_specs=[vmem, vmem],
        out_specs=(vmem, vmem, vmem),
        scratch_shapes=[
            pltpu.VMEM((slots, LANES), jnp.float32),
            pltpu.VMEM((2 * GROUP * 8 * points // LANES, LANES), jnp.float32),
            pltpu.SMEM((slots // LANES, LANES), jnp.int32),
            pltpu.SMEM((slots // GROUP + 2,), jnp.int32),
            pltpu.SemaphoreType.DMA,
        ],
        name="pairs",
    )(incoming, tables)
    returned = lax.all_to_all(mine, "tile", split_axis=0, concat_axis=0, tiled=True)
    scans = jnp.arange(SCANS_DEV, dtype=jnp.int32)
    tgt_onehot = (owner_scan.reshape(slots)[:, None] == scans[None, :]).astype(jnp.float32)
    contract = (((0,), (0,)), ((), ()))
    sums = lax.dot_general(terms[:, HALF : 2 * HALF], tgt_onehot, contract, precision=PRECISE)
    places = slot_scan.reshape(slots // fold, fold)
    onehot = (places[:, :, None] == scans[None, None, :]).astype(jnp.float32)
    spread = lax.dot_general(returned, onehot.reshape(-1, fold * SCANS_DEV), contract, precision=PRECISE)
    for at in range(fold):
        sums = sums + spread[at * HALF : (at + 1) * HALF, at * SCANS_DEV : (at + 1) * SCANS_DEV]
    totals = lax.psum(sums, "grp")
    return solve_poses(totals)


def solution(mesh):
    in_specs = (
        P("grp", None, "tile"),
        P("grp", "tile", None),
        P("grp", "tile"),
        P("grp", "tile"),
        P(None, "tile"),
        P(None, "tile"),
    )
    return jax.shard_map(body, mesh=mesh, in_specs=in_specs, out_specs=P(None, "tile"), check_vma=False)
```
